512 devices in a mesh: dp: 64 (over z_lo, y, core), expert: 8 (over x, z_hi).
Axes of the slice: x: 4, y: 8, z: 8 (z_hi: 2, z_lo: 4; z = z_hi * 4 + z_lo), core: 2. Of those that a mesh axis runs over, the one named last changes fastest.
Arguments:
- tokens: bfloat16 [131072, 1024], P(('dp', 'expert')), may hold values from -6 to 6
- expert_ids: int32 [131072], P(('dp', 'expert')), may hold values from 0 to 7
- slots: int32 [131072], P(('dp', 'expert')), may hold values from -1 to 39, as said below
- router: bfloat16 [1024, 8], replicated, may hold values from -0.1875 to 0.1875
- w_in: bfloat16 [8, 1024, 2048], P('expert', 'dp'), may hold values from -0.1875 to 0.1875
- w_out: bfloat16 [8, 2048, 1024], P('expert', None, 'dp'), may hold values from -0.125 to 0.125
- texts: bfloat16 [2048, 1024], P(('dp', 'expert')), may hold values from -6 to 6
Outputs:
- d_tokens: bfloat16 [131072, 1024], P(('dp', 'expert'))
- d_texts: float32 [2048, 1024], P(('dp', 'expert'))
- router_grad: float32 [1024, 8], replicated
The draws below stay inside these ranges and needn't reach their ends.
Inputs may be any that keep to these rules, and one draw needn't show every extreme that they name: Within each block of 256 tokens (one device's), the tokens of each expert hold slots 0, 1, 2, ... in token order until 40, and -1 after. On every index of dp, some expert receives all 40 slots from each of the 8 blocks of that index.
All inputs are finite; a program needn't handle non-finite values.
Results may differ from the reference program's by a relative error of at most 0.0064.
Values may be sent and summed in bfloat16 or wider, within the bound.
No kernel may reach another device: no remote copies, remote signals or barrier semaphores. Data moves between devices by JAX's collectives and lax.ppermute only.
A program may use at most 64 MiB of HBM per device.

```python
import jax
import jax.numpy as jnp
from jax import lax

D = 1024
FFW = 2048
PATCH = 64
IMG_DEV = 4
EXPERTS = 8
SOURCES = 8
BLOCKS = 512
TOK_DEV = 256
CAP = 40
IMAGES = 2048
TOKENS = 131072
N_DP = 64


def route_tables(key):
    base = jax.random.fold_in(key, 11)
    row_key, pick_key, order_key = jax.random.split(base, 3)
    hot_rows = jax.random.randint(row_key, (BLOCKS // SOURCES,), 0, EXPERTS)
    hot_blocks = jnp.repeat(hot_rows, SOURCES)
    picked = jax.random.randint(pick_key, (BLOCKS, TOK_DEV), 0, EXPERTS)
    orders = jax.vmap(lambda inner: jax.random.permutation(inner, TOK_DEV))(jax.random.split(order_key, BLOCKS))
    forced = orders < CAP + CAP // 5 + 1
    assigned = jnp.where(forced, hot_blocks[:, None], picked).astype(jnp.int32)
    onehot = (assigned[:, :, None] == jnp.arange(EXPERTS, dtype=jnp.int32)[None, None, :]).astype(jnp.int32)
    running = jnp.cumsum(onehot, axis=1) - 1
    ranks = jnp.sum(running * onehot, axis=2)
    placed = jnp.where(ranks < CAP, ranks, -1).astype(jnp.int32)
    return (assigned.reshape(-1), placed.reshape(-1))


def draw_expert_ids(key, part):
    return route_tables(key)[0]


def draw_slots(key, part):
    return route_tables(key)[1]


def shard_levels(key, shape, cuts, least, top_value):
    level, own = 1.0, jax.random.fold_in(key, 6)
    for axis_at, parts in cuts:
        draws = jnp.exp(jax.random.uniform(jax.random.fold_in(own, axis_at), (parts,), jnp.float32, least / len(cuts), top_value / len(cuts)))
        level = level * jnp.repeat(draws, shape[axis_at] // parts).reshape([-1 if axis == axis_at else 1 for axis in range(len(shape))])
    return level


def noise(rng, dims, scale, most, cuts=(), kind=jnp.bfloat16):
    values = scale * jax.random.normal(rng, dims, jnp.float32)
    if cuts:
        values = values * shard_levels(rng, dims, cuts, -0.22, 0.18)
    return jnp.clip(values, -most, most).astype(kind)


def setup_inputs(seed: int = 0) -> dict:
    arg_keys = jax.random.split(jax.random.key(seed), 8)
    tokens = noise(arg_keys[0], (TOKENS, D), 1.0, 6.0, ((0, 512),))
    expert_ids = draw_expert_ids(jax.random.fold_in(arg_keys[7], 71), 0)
    slots = draw_slots(jax.random.fold_in(arg_keys[7], 71), 0)
    router = noise(arg_keys[3], (D, EXPERTS), D ** -0.5, 0.1875)
    w_in = noise(arg_keys[4], (EXPERTS, D, FFW), D ** -0.5, 0.1875, ((0, 8), (1, 64)))
    w_out = noise(arg_keys[5], (EXPERTS, FFW, D), FFW ** -0.5, 0.125, ((0, 8), (2, 64)))
    texts = noise(arg_keys[6], (IMAGES, D), 1.0, 6.0, ((0, 512),))
    return dict(tokens=tokens, expert_ids=expert_ids, slots=slots, router=router, w_in=w_in, w_out=w_out, texts=texts)


highest = lax.Precision.HIGHEST
temper = 10.0
offset = -2.0
loss_scale = 256.0
epsilon = 1e-06

def gelu_slope(hidden):
    result, pullback = jax.vjp(lambda inputs: jax.nn.gelu(inputs, approximate=True), hidden)
    return pullback(jnp.ones_like(hidden))[0]

def contract_last(left, right):
    return lax.dot_general(left, right, (((1,), (1,)), ((), ())), preferred_element_type=jnp.float32)

def reference(tokens, expert_ids, slots, router, w_in, w_out, texts):
    is_kept = slots >= 0
    kept_float = is_kept.astype(jnp.float32)
    columns = jnp.arange(EXPERTS, dtype=jnp.int32)
    chosen = (expert_ids[:, None] == columns[None, :]).astype(jnp.float32)
    logits = jnp.dot(tokens, router, preferred_element_type=jnp.float32)
    gate_values = jax.nn.sigmoid(lax.optimization_barrier(jnp.sum(logits * chosen, axis=1)))
    block_of = jnp.arange(TOKENS, dtype=jnp.int32) // TOK_DEV
    slot_total = BLOCKS * EXPERTS * CAP
    places = jnp.where(is_kept, (block_of * EXPERTS + expert_ids) * CAP + slots, slot_total).astype(jnp.int32)
    safe_places = jnp.minimum(places, slot_total - 1)

    def by_expert(rows):
        buffer = jnp.zeros((slot_total, D), jnp.bfloat16).at[places].set(rows, mode='drop')
        return buffer.reshape(BLOCKS, EXPERTS, CAP, D).transpose(1, 0, 2, 3).reshape(EXPERTS, BLOCKS * CAP, D)

    def to_tokens(stacked):
        flat = stacked.reshape(EXPERTS, BLOCKS, CAP, D).transpose(1, 0, 2, 3).reshape(slot_total, D)
        return jnp.where(is_kept[:, None], flat[safe_places].astype(jnp.float32), 0.0)
    routed = by_expert(tokens)

    def forward(items):
        inputs, in_matrix, out_matrix = items
        hidden = jnp.dot(inputs, in_matrix, preferred_element_type=jnp.float32)
        active = jax.nn.gelu(hidden, approximate=True).astype(jnp.bfloat16)
        return jnp.dot(active, out_matrix, preferred_element_type=jnp.float32).astype(jnp.bfloat16)
    combined = to_tokens(lax.map(forward, (routed, w_in, w_out)))
    branch = gate_values[:, None] * combined
    pooled = lax.optimization_barrier(jnp.mean(branch.reshape(IMAGES, PATCH, D), axis=1))
    pooled_scale = lax.rsqrt(lax.optimization_barrier(jnp.sum(pooled * pooled, axis=1, keepdims=True)) + epsilon)
    unit_img = pooled * pooled_scale
    text_float = texts.astype(jnp.float32)
    text_scale = lax.rsqrt(lax.optimization_barrier(jnp.sum(text_float * text_float, axis=1, keepdims=True)) + epsilon)
    unit_txt = text_float * text_scale
    block_shape = (N_DP, SOURCES, IMG_DEV, D)
    image_blocks = unit_img.reshape(block_shape)
    text_blocks = unit_txt.reshape(block_shape)
    prev_text = jnp.roll(text_blocks, 1, axis=0)
    diagonal = jnp.eye(IMG_DEV, dtype=jnp.float32)
    own_scores = temper * jnp.einsum('abid,abjd->abij', image_blocks, text_blocks, precision=highest) + offset
    next_scores = temper * jnp.einsum('abid,abjd->abij', image_blocks, prev_text, precision=highest) + offset
    own_grad = loss_scale * (jax.nn.sigmoid(own_scores) - diagonal)
    next_grad = loss_scale * jax.nn.sigmoid(next_scores)
    grad_image = temper * (jnp.einsum('abij,abjd->abid', own_grad, text_blocks, precision=highest) + jnp.einsum('abij,abjd->abid', next_grad, prev_text, precision=highest))
    grad_text_own = temper * jnp.einsum('abij,abid->abjd', own_grad, image_blocks, precision=highest)
    grad_text_next = temper * jnp.einsum('abij,abid->abjd', next_grad, image_blocks, precision=highest)
    grad_text = (grad_text_own + jnp.roll(grad_text_next, -1, axis=0)).reshape(IMAGES, D)
    d_texts = (grad_text - unit_txt * lax.optimization_barrier(jnp.sum(unit_txt * grad_text, axis=1, keepdims=True))) * text_scale
    grad_image = grad_image.reshape(IMAGES, D)
    grad_pooled = (grad_image - unit_img * lax.optimization_barrier(jnp.sum(unit_img * grad_image, axis=1, keepdims=True))) * pooled_scale
    grad_branch = jnp.repeat(grad_pooled, PATCH, axis=0) / PATCH
    grad_combined = jnp.where(is_kept[:, None], gate_values[:, None] * grad_branch, 0.0).astype(jnp.bfloat16)
    grad_gate = lax.optimization_barrier(jnp.sum(grad_branch * combined, axis=1))
    grad_logits = chosen * (grad_gate * gate_values * (1.0 - gate_values) * kept_float)[:, None]
    router_grad = jnp.dot(tokens.astype(jnp.float32).T, grad_logits, precision=highest)
    router_part = jnp.dot(grad_logits, router.astype(jnp.float32).T, precision=highest)
    routed_grads = by_expert(grad_combined)

    def backward(items):
        inputs, grads, in_matrix, out_matrix = items
        hidden = jnp.dot(inputs, in_matrix, preferred_element_type=jnp.float32)
        grad_hidden = (contract_last(grads, out_matrix) * gelu_slope(hidden)).astype(jnp.bfloat16)
        return contract_last(grad_hidden, in_matrix).astype(jnp.bfloat16)
    grad_routed = to_tokens(lax.map(backward, (routed, routed_grads, w_in, w_out)))
    d_tokens = (grad_routed + router_part).astype(jnp.bfloat16)
    return (d_tokens, d_texts, router_grad)
```

```python
import functools

import jax
import jax.numpy as jnp
from jax import lax
from jax.experimental import pallas as pl
from jax.experimental.pallas import tpu as pltpu
from jax.sharding import Mesh
from jax.sharding import PartitionSpec as P


highest = lax.Precision.HIGHEST
temper = 10.0
offset = -2.0
loss_scale = 256.0
epsilon = 1e-06

AXES = ("a", "b", "y", "c", "x", "zh")
DP = ("a", "b", "y", "c")
GROUP = ("x", "b")
OWNERS = ("a", "y", "c", "zh")
RING = ("a", "b", "zh")

ANY = pl.BlockSpec(memory_space=pl.ANY)
VMEM = pl.BlockSpec(memory_space=pltpu.VMEM)
SMEM = pl.BlockSpec(memory_space=pltpu.SMEM)


def ring_index(z):
    return (z // 2) % 2 * 4 + z % 2 * 2 + z // 4


def depth_round(k):
    return [
        (ring_index(4 * p + i), ring_index(2 * ((i + k) % 4) + p))
        for p in range(2)
        for i in range(4)
    ]


def ring_step(d):
    return [(i, (i + d) % 8) for i in range(8)]


def swap_cores(block):
    return lax.ppermute(block, "c", [(0, 1), (1, 0)])


def contract_last(left, right):
    return lax.dot_general(
        left, right, (((1,), (1,)), ((), ())), preferred_element_type=jnp.float32
    )


def start_copies(where, parts, refs, w_ref, sem, kind):
    y, j, c = where[0], where[1], where[2]
    for which, lead, k, far, other in parts:
        at_y = lax.rem(y + far, 8)
        at_zl = lax.rem(j - k + 4, 4)
        core = 1 - c if other else c
        row = pl.multiple_of(((at_zl * 8 + at_y) * 2 + core) * 16, 16)
        src = refs[which].at[lead, pl.ds(kind * 16, 16), :]
        pltpu.make_async_copy(src, w_ref.at[pl.ds(row, 16), :], sem).start()


def wait_all(w_ref, sem):
    pltpu.make_async_copy(w_ref, w_ref, sem).wait()


def forward_kernel(parts, count, where, x_ref, *rest):
    refs, (hid_ref, out_ref, win, wout, act, sems) = rest[:count], rest[count:]
    start_copies(where, parts, refs, win, sems.at[0], 0)
    start_copies(where, parts, refs, wout, sems.at[1], 1)
    wait_all(win, sems.at[0])

    def up(n, carry):
        at = pl.ds(pl.multiple_of(n * 512, 512), 512)
        hidden = jnp.dot(x_ref[...], win[:, at], preferred_element_type=jnp.float32)
        hid_ref[:, at] = hidden
        act[:, at] = jax.nn.gelu(hidden, approximate=True).astype(jnp.bfloat16)
        return carry

    lax.fori_loop(0, 4, up, 0)
    wait_all(wout, sems.at[1])

    for n in range(4):
        at = slice(n * 256, n * 256 + 256)
        out_ref[:, at] = contract_last(act[...], wout[at, :]).astype(jnp.bfloat16)


def gelu_slope(hidden):
    scale = 0.7978845608028654
    square = hidden * hidden
    bent = jnp.tanh(scale * (hidden + 0.044715 * (square * hidden)))
    inner = scale * (1.0 + 3.0 * 0.044715 * square)
    return 0.5 * (1.0 + bent) + 0.5 * hidden * (1.0 - bent * bent) * inner


def backward_kernel(parts, count, where, dy_ref, hid_ref, *rest):
    refs, (dx_ref, win, wout, dhid, sems) = rest[:count], rest[count:]
    start_copies(where, parts, refs, wout, sems.at[1], 1)
    start_copies(where, parts, refs, win, sems.at[0], 0)
    wait_all(wout, sems.at[1])

    def down(n, carry):
        at = pl.ds(pl.multiple_of(n * 512, 512), 512)
        grad = jnp.dot(dy_ref[...], wout[:, at], preferred_element_type=jnp.float32)
        dhid[:, at] = (grad * gelu_slope(hid_ref[:, at])).astype(jnp.bfloat16)
        return carry

    lax.fori_loop(0, 4, down, 0)
    wait_all(win, sems.at[0])
    for n in range(4):
        at = slice(n * 256, n * 256 + 256)
        dx_ref[:, at] = contract_last(dhid[...], win[at, :]).astype(jnp.bfloat16)


def gathered_weights(w_in, w_out):
    own = jnp.concatenate([w_in[0], w_out[0].T], axis=0)
    rounds = [lax.ppermute(own, RING, depth_round(k)) for k in range(4)]
    mine = jnp.stack(rounds)
    arrays, parts = [], []

    def add(array, entries, other):
        parts.extend((len(arrays), i, k, far, other) for i, (k, far) in enumerate(entries))
        arrays.append(array)

    def both(blocks):
        pool, table = [], []
        for block, entries in blocks:
            add(block, entries, False)
            pool.append(block)
            table.extend(entries)
        add(swap_cores(pool[0] if len(pool) == 1 else jnp.concatenate(pool)), table, True)

    rows = lambda far, ks=range(4): [(k, far % 8) for k in ks]
    plus = lax.ppermute(mine, "y", ring_step(1))
    minus = lax.ppermute(mine, "y", ring_step(-1))
    both([(mine, rows(0))])
    plus2 = lax.ppermute(plus, "y", ring_step(1))
    minus2 = lax.ppermute(minus, "y", ring_step(-1))
    both([(plus, rows(-1)), (minus, rows(1))])
    plus3 = lax.ppermute(plus2, "y", ring_step(1))
    minus3 = lax.ppermute(minus2, "y", ring_step(-1))
    both([(plus2, rows(-2)), (minus2, rows(2))])
    plus4 = lax.ppermute(plus3[:2], "y", ring_step(1))
    minus4 = lax.ppermute(minus3[2:], "y", ring_step(-1))
    both([(plus3, rows(-3)), (minus3, rows(3))])
    both([(plus4, rows(4, (0, 1))), (minus4, rows(4, (2, 3)))])
    return arrays, parts


def share(block, axes, count):
    return lax.all_to_all(
        jnp.broadcast_to(block[None], (count,) + block.shape), axes, 0, 0, tiled=True
    )


def unit_rows(matrix):
    scales = lax.rsqrt(jnp.sum(matrix * matrix, axis=1, keepdims=True) + epsilon)
    return matrix * scales, scales


def body(tokens, expert_ids, slots, router, w_in, w_out, texts):
    tok_count, width = tokens.shape
    experts = router.shape[1]
    capacity = 5 * tok_count // (4 * experts)
    images = texts.shape[0]
    patch = tok_count // images
    slot_total = experts * capacity
    rows = slot_total
    hidden_width = w_in.shape[2]
    f32, bf16 = jnp.float32, jnp.bfloat16
    me = lax.axis_index(GROUP)
    pictures = experts * images

    before = lax.ppermute(texts, DP, [(i, (i + 1) % 64) for i in range(64)])
    arrays, parts = gathered_weights(w_in, w_out)

    places = jnp.where(slots >= 0, expert_ids * capacity + slots, slot_total)
    picks = (jnp.arange(slot_total, dtype=jnp.int32)[:, None] == places[None, :]).astype(bf16)
    image_of = me * images + jnp.arange(tok_count, dtype=jnp.int32) // patch
    marks = (image_of[:, None] == jnp.arange(128, dtype=jnp.int32)[None, :]).astype(bf16)
    wide = jnp.concatenate([tokens, marks], axis=1)
    send = jnp.dot(picks, wide, preferred_element_type=f32).astype(bf16)
    pair = jnp.pad(jnp.concatenate([texts, before], axis=0), ((0, 0), (0, 128)))
    send = jnp.concatenate(
        [
            send.reshape(experts, capacity, width + 128),
            jnp.broadcast_to(pair[None], (experts,) + pair.shape),
        ],
        axis=1,
    )
    arrived = lax.all_to_all(send, GROUP, 0, 0, tiled=True)
    routed = arrived[:, :capacity, :width].reshape(rows, width)
    marked = arrived[:, :capacity, width : width + pictures].reshape(rows, pictures)
    own_text = arrived[:, capacity : capacity + images, :width].reshape(pictures, width)
    old_text = arrived[:, capacity + images :, :width].reshape(pictures, width)

    mine = (jnp.arange(experts, dtype=jnp.int32) == me).astype(f32)
    logits = jnp.dot(routed, router, preferred_element_type=f32)
    gates = jax.nn.sigmoid(jnp.sum(logits * mine[None, :], axis=1))
    marked = marked.astype(f32)
    router_row = jnp.sum(router.astype(f32) * mine[None, :], axis=1)
    text_units, text_scales = unit_rows(
        jnp.concatenate([own_text, old_text], axis=0).astype(f32)
    )

    y_at, c_at = lax.axis_index("y"), lax.axis_index("c")
    where = jnp.stack([y_at, 2 * lax.axis_index("zh") + lax.axis_index("a"), c_at])
    where = where.astype(jnp.int32)
    weight_scratch = [pltpu.VMEM((width, hidden_width), bf16)] * 2
    hidden, out = pl.pallas_call(
        functools.partial(forward_kernel, parts, len(arrays)),
        out_shape=(
            jax.ShapeDtypeStruct((rows, hidden_width), f32),
            jax.ShapeDtypeStruct((rows, width), bf16),
        ),
        in_specs=[SMEM, VMEM] + [ANY] * len(arrays),
        out_specs=(VMEM, VMEM),
        scratch_shapes=weight_scratch
        + [pltpu.VMEM((rows, hidden_width), bf16), pltpu.SemaphoreType.DMA((2,))],
        name="forward",
    )(where, routed, *arrays)

    out_float = out.astype(f32)
    weights = marked * gates[:, None]
    part = lax.dot_general(
        weights, out_float, (((0,), (0,)), ((), ())), precision=highest
    )
    shared = share(part.astype(bf16), GROUP, experts)
    pooled = jnp.sum(shared.astype(f32), axis=0) / patch

    units, pooled_scale = unit_rows(pooled)
    scores = temper * lax.dot_general(
        units, text_units, (((1,), (1,)), ((), ())), precision=highest
    ) + offset
    at_row = jnp.arange(pictures, dtype=jnp.int32)[:, None]
    at_col = jnp.arange(2 * pictures, dtype=jnp.int32)[None, :]
    paired = at_row // images == (at_col % pictures) // images
    label = (at_row == at_col).astype(f32)
    pulls = jnp.where(paired, loss_scale * (jax.nn.sigmoid(scores) - label), 0.0)
    grad_image = temper * jnp.dot(pulls, text_units, precision=highest)
    grad_pooled = (
        grad_image - units * jnp.sum(units * grad_image, axis=1, keepdims=True)
    ) * pooled_scale
    grad_branch = grad_pooled / patch

    spread = jnp.dot(marked, grad_branch, precision=highest)
    grad_out = (gates[:, None] * spread).astype(bf16)
    grad_gate = jnp.sum(spread * out_float, axis=1)
    grad_logit = grad_gate * gates * (1.0 - gates)
    column = jnp.dot(grad_logit[None, :], routed.astype(f32), precision=highest)
    columns = share(column.reshape(8, width // 8), OWNERS, 64)
    column = jnp.sum(columns, axis=0).reshape(1, width)
    high = column.astype(bf16)
    rest = column - high.astype(f32)
    middle = rest.astype(bf16)
    low = (rest - middle.astype(f32)).astype(bf16)

    grad_routed = pl.pallas_call(
        functools.partial(backward_kernel, parts, len(arrays)),
        out_shape=jax.ShapeDtypeStruct((rows, width), bf16),
        in_specs=[SMEM, VMEM, VMEM] + [ANY] * len(arrays),
        out_specs=VMEM,
        scratch_shapes=weight_scratch
        + [pltpu.VMEM((rows, hidden_width), bf16), pltpu.SemaphoreType.DMA((2,))],
        name="backward",
    )(where, grad_out, hidden, *arrays)
    grad_rows = grad_routed.astype(f32) + grad_logit[:, None] * router_row[None, :]
    tail = jnp.concatenate([high, middle, low, jnp.zeros((5, width), bf16)], axis=0)
    back = jnp.concatenate(
        [
            grad_rows.astype(bf16).reshape(experts, capacity, width),
            jnp.broadcast_to(tail[None], (experts,) + tail.shape),
        ],
        axis=1,
    )
    back = lax.all_to_all(back, GROUP, 0, 0, tiled=True)
    d_tokens = lax.dot_general(
        picks,
        back[:, :capacity].reshape(slot_total, width),
        (((0,), (0,)), ((), ())),
        preferred_element_type=f32,
    ).astype(bf16)
    router_grad = jnp.sum(back[:, capacity : capacity + 3].astype(f32), axis=1).T

    text_pulls = temper * lax.dot_general(
        pulls, units, (((0,), (0,)), ((), ())), precision=highest
    )
    own_pull = lax.dynamic_slice_in_dim(text_pulls, me * images, images)
    old_pull = lax.dynamic_slice_in_dim(text_pulls, pictures + me * images, images)
    own_unit = lax.dynamic_slice_in_dim(text_units, me * images, images)
    own_scale = lax.dynamic_slice_in_dim(text_scales, me * images, images)
    grad_text = own_pull + lax.ppermute(
        old_pull, DP, [((i + 1) % 64, i) for i in range(64)]
    )
    d_texts = (
        grad_text - own_unit * jnp.sum(own_unit * grad_text, axis=1, keepdims=True)
    ) * own_scale
    return d_tokens, d_texts, router_grad


def solution(mesh):
    fine = Mesh(mesh.devices.reshape(2, 2, 8, 2, 4, 2), AXES)
    block = P(AXES, None)
    flat = P(AXES)
    in_specs = (
        block,
        flat,
        flat,
        P(),
        P(("x", "zh"), DP, None),
        P(("x", "zh"), None, DP),
        block,
    )
    out_specs = (block, block, P())
    return jax.shard_map(body, mesh=fine, in_specs=in_specs, out_specs=out_specs, check_vma=False)
```

```python
import functools

import jax
import jax.numpy as jnp
from jax import lax
from jax.experimental import pallas as pl
from jax.experimental.pallas import tpu as pltpu
from jax.sharding import Mesh
from jax.sharding import PartitionSpec as P


highest = lax.Precision.HIGHEST
temper = 10.0
offset = -2.0
loss_scale = 256.0
epsilon = 1e-06

AXES = ("a", "b", "y", "c", "x", "zh")
DP = ("a", "b", "y", "c")
GROUP = ("x", "b")
OWNERS = ("a", "y", "c", "zh")
RING = ("a", "b", "zh")

ANY = pl.BlockSpec(memory_space=pl.ANY)
VMEM = pl.BlockSpec(memory_space=pltpu.VMEM)
SMEM = pl.BlockSpec(memory_space=pltpu.SMEM)


def ring_index(z):
    return (z // 2) % 2 * 4 + z % 2 * 2 + z // 4


def depth_round(k):
    return [
        (ring_index(4 * p + i), ring_index(2 * ((i + k) % 4) + p))
        for p in range(2)
        for i in range(4)
    ]


def ring_step(d):
    return [(i, (i + d) % 8) for i in range(8)]


def swap_cores(block):
    return lax.ppermute(block, "c", [(0, 1), (1, 0)])


def contract_last(left, right):
    return lax.dot_general(
        left, right, (((1,), (1,)), ((), ())), preferred_element_type=jnp.float32
    )


def start_copies(where, parts, refs, w_ref, sem, kind):
    y, j, c = where[0], where[1], where[2]
    for which, lead, k, far, other in parts:
        at_y = lax.rem(y + far, 8)
        at_zl = lax.rem(j - k + 4, 4)
        core = 1 - c if other else c
        row = pl.multiple_of(((at_zl * 8 + at_y) * 2 + core) * 16, 16)
        src = refs[which].at[lead, pl.ds(kind * 16, 16), :]
        pltpu.make_async_copy(src, w_ref.at[pl.ds(row, 16), :], sem).start()


def wait_all(w_ref, sem):
    pltpu.make_async_copy(w_ref, w_ref, sem).wait()


def forward_kernel(parts, count, where, x_ref, mix_ref, *rest):
    refs, (hid_ref, out_ref, part_ref, win, wout, act, sems) = rest[:count], rest[count:]
    start_copies(where, parts, refs, win, sems.at[0], 0)
    start_copies(where, parts, refs, wout, sems.at[1], 1)
    wait_all(win, sems.at[0])
    for n in range(4):
        at = slice(n * 512, n * 512 + 512)
        hidden = jnp.dot(x_ref[...], win[:, at], preferred_element_type=jnp.float32)
        hid_ref[:, at] = hidden
        act[:, at] = jax.nn.gelu(hidden, approximate=True).astype(jnp.bfloat16)
    wait_all(wout, sems.at[1])
    for n in range(4):
        at = slice(n * 256, n * 256 + 256)
        out = contract_last(act[...], wout[at, :]).astype(jnp.bfloat16)
        out_ref[:, at] = out
        part = jnp.dot(
            mix_ref[...],
            out.astype(jnp.float32),
            precision=highest,
            preferred_element_type=jnp.float32,
        ).astype(jnp.bfloat16)
        for member in range(part_ref.shape[0]):
            part_ref[member, :, at] = part


def gelu_slope(hidden):
    scale = 0.7978845608028654
    square = hidden * hidden
    bent = jnp.tanh(scale * (hidden + 0.044715 * (square * hidden)))
    inner = scale * (1.0 + 3.0 * 0.044715 * square)
    return 0.5 * (1.0 + bent) + 0.5 * hidden * (1.0 - bent * bent) * inner


def backward_kernel(parts, count, where, dy_ref, hid_ref, grad_logit, router_row, *rest):
    refs, (back_ref, win, wout, dhid, sems) = rest[:count], rest[count:]
    start_copies(where, parts, refs, wout, sems.at[1], 1)
    start_copies(where, parts, refs, win, sems.at[0], 0)
    wait_all(wout, sems.at[1])
    for n in range(4):
        at = slice(n * 512, n * 512 + 512)
        grad = jnp.dot(dy_ref[...], wout[:, at], preferred_element_type=jnp.float32)
        dhid[:, at] = (grad * gelu_slope(hid_ref[:, at])).astype(jnp.bfloat16)
    wait_all(win, sems.at[0])
    members, _, width = back_ref.shape
    capacity = dhid.shape[0] // members
    back_ref[:, capacity:, :] = jnp.zeros((members, 8, width), jnp.bfloat16)
    for n in range(4):
        at = slice(n * 256, n * 256 + 256)
        moved = contract_last(dhid[...], win[at, :]).astype(jnp.bfloat16)
        rows = moved.astype(jnp.float32) + grad_logit[...] * router_row[:, at]
        for member in range(members):
            block = rows[member * capacity : (member + 1) * capacity]
            back_ref[member, :capacity, at] = block.astype(jnp.bfloat16)


def gathered_weights(w_in, w_out, settle):
    own = jnp.concatenate([w_in[0], w_out[0].T], axis=0)
    rounds = [lax.ppermute(own, RING, depth_round(k)) for k in range(4)]
    mine = jnp.stack(rounds)
    arrays, parts = [], []

    def add(array, entries, other):
        parts.extend((len(arrays), i, k, far, other) for i, (k, far) in enumerate(entries))
        arrays.append(array)

    def both(blocks):
        pool, table = [], []
        for block, entries in blocks:
            add(block, entries, False)
            pool.append(block)
            table.extend(entries)
        add(swap_cores(pool[0] if len(pool) == 1 else jnp.concatenate(pool)), table, True)

    rows = lambda far, ks=range(4): [(k, far % 8) for k in ks]
    plus = lax.ppermute(mine, "y", ring_step(1))
    minus = lax.ppermute(mine, "y", ring_step(-1))
    both([(mine, rows(0))])
    plus2 = lax.ppermute(plus, "y", ring_step(1))
    minus2 = lax.ppermute(minus, "y", ring_step(-1))
    both([(plus, rows(-1)), (minus, rows(1))])
    plus3 = lax.ppermute(plus2, "y", ring_step(1))
    minus3 = lax.ppermute(minus2, "y", ring_step(-1))
    both([(plus2, rows(-2)), (minus2, rows(2))])
    plus3, minus3, settled = lax.optimization_barrier((plus3, minus3, settle()))
    plus4 = lax.ppermute(plus3[:2], "y", ring_step(1))
    minus4 = lax.ppermute(minus3[2:], "y", ring_step(-1))
    both([(plus3, rows(-3)), (minus3, rows(3))])
    both([(plus4, rows(4, (0, 1))), (minus4, rows(4, (2, 3)))])
    return arrays, parts, settled


def share(block, axes, count):
    return lax.all_to_all(
        jnp.broadcast_to(block[None], (count,) + block.shape), axes, 0, 0, tiled=True
    )


def unit_rows(matrix):
    scales = lax.rsqrt(jnp.sum(matrix * matrix, axis=1, keepdims=True) + epsilon)
    return matrix * scales, scales


def body(tokens, expert_ids, slots, router, w_in, w_out, texts):
    tok_count, width = tokens.shape
    experts = router.shape[1]
    capacity = 5 * tok_count // (4 * experts)
    images = texts.shape[0]
    patch = tok_count // images
    slot_total = experts * capacity
    rows = slot_total
    hidden_width = w_in.shape[2]
    f32, bf16 = jnp.float32, jnp.bfloat16
    me = lax.axis_index(GROUP)
    pictures = experts * images

    before = lax.ppermute(texts, DP, [(i, (i + 1) % 64) for i in range(64)])
    places = jnp.where(slots >= 0, expert_ids * capacity + slots, slot_total)
    picks = (jnp.arange(slot_total, dtype=jnp.int32)[:, None] == places[None, :]).astype(bf16)
    image_of = me * images + jnp.arange(tok_count, dtype=jnp.int32) // patch
    marks = (image_of[:, None] == jnp.arange(128, dtype=jnp.int32)[None, :]).astype(bf16)
    wide = jnp.concatenate([tokens, marks], axis=1)
    send = jnp.dot(picks, wide, preferred_element_type=f32).astype(bf16)
    pair = jnp.pad(jnp.concatenate([texts, before], axis=0), ((0, 0), (0, 128)))
    send = jnp.concatenate(
        [
            send.reshape(experts, capacity, width + 128),
            jnp.broadcast_to(pair[None], (experts,) + pair.shape),
        ],
        axis=1,
    )
    mine = (jnp.arange(experts, dtype=jnp.int32) == me).astype(f32)
    y_at, c_at = lax.axis_index("y"), lax.axis_index("c")
    j_at = 2 * lax.axis_index("zh") + lax.axis_index("a")
    place = jnp.arange(3, dtype=jnp.int32)
    where = jnp.where(place == 0, y_at, jnp.where(place == 1, j_at, c_at)).astype(jnp.int32)

    def settle():
        arrived = lax.all_to_all(send, GROUP, 0, 0, tiled=True)
        routed = arrived[:, :capacity, :width].reshape(rows, width)
        marked = arrived[:, :capacity, width : width + pictures].reshape(rows, pictures)
        marked = marked.astype(f32)
        own_text = arrived[:, capacity : capacity + images, :width].reshape(pictures, width)
        old_text = arrived[:, capacity + images :, :width].reshape(pictures, width)
        logits = jnp.dot(routed, router, preferred_element_type=f32)
        gates = jax.nn.sigmoid(jnp.sum(logits * mine[None, :], axis=1))
        router_row = jnp.sum(router.astype(f32) * mine[None, :], axis=1)[None, :]
        mix = (marked * gates[:, None]).T
        text_units, text_scales = unit_rows(
            jnp.concatenate([own_text, old_text], axis=0).astype(f32)
        )
        at_row = jnp.arange(pictures, dtype=jnp.int32)[:, None]
        at_col = jnp.arange(2 * pictures, dtype=jnp.int32)[None, :]
        paired = (at_row // images == (at_col % pictures) // images).astype(f32)
        label = (at_row == at_col).astype(f32)
        return routed, marked, gates, router_row, mix, text_units, text_scales, where, paired, label

    arrays, parts, settled = gathered_weights(w_in, w_out, settle)
    routed, marked, gates, router_row, mix, text_units, text_scales, where, paired, label = settled

    weight_scratch = [pltpu.VMEM((width, hidden_width), bf16)] * 2
    hidden, out, part = pl.pallas_call(
        functools.partial(forward_kernel, parts, len(arrays)),
        out_shape=(
            jax.ShapeDtypeStruct((rows, hidden_width), f32),
            jax.ShapeDtypeStruct((rows, width), bf16),
            jax.ShapeDtypeStruct((experts, pictures, width), bf16),
        ),
        in_specs=[SMEM, VMEM, VMEM] + [ANY] * len(arrays),
        out_specs=(VMEM, VMEM, VMEM),
        scratch_shapes=weight_scratch
        + [pltpu.VMEM((rows, hidden_width), bf16), pltpu.SemaphoreType.DMA((2,))],
        name="forward",
    )(where, routed, mix, *arrays)

    shared = lax.all_to_all(part, GROUP, 0, 0, tiled=True)
    out_float = out.astype(f32)
    pooled = jnp.sum(shared.astype(f32), axis=0) / patch

    units, pooled_scale = unit_rows(pooled)
    scores = temper * lax.dot_general(
        units, text_units, (((1,), (1,)), ((), ())), precision=highest
    ) + offset
    pulls = paired * (loss_scale * (jax.nn.sigmoid(scores) - label))
    grad_image = temper * jnp.dot(pulls, text_units, precision=highest)
    grad_pooled = (
        grad_image - units * jnp.sum(units * grad_image, axis=1, keepdims=True)
    ) * pooled_scale
    grad_branch = grad_pooled / patch

    spread = jnp.dot(marked, grad_branch, precision=highest)
    grad_out = (gates[:, None] * spread).astype(bf16)
    grad_gate = jnp.sum(spread * out_float, axis=1)
    grad_logit = grad_gate * gates * (1.0 - gates)
    column = jnp.dot(grad_logit[None, :], routed.astype(f32), precision=highest)
    columns = share(column.reshape(8, width // 8), OWNERS, 64)
    column = jnp.sum(columns, axis=0).reshape(1, width)
    high = column.astype(bf16)
    rest = column - high.astype(f32)
    middle = rest.astype(bf16)
    low = (rest - middle.astype(f32)).astype(bf16)

    back = pl.pallas_call(
        functools.partial(backward_kernel, parts, len(arrays)),
        out_shape=jax.ShapeDtypeStruct((experts, capacity + 8, width), bf16),
        in_specs=[SMEM, VMEM, VMEM, VMEM, VMEM] + [ANY] * len(arrays),
        out_specs=VMEM,
        scratch_shapes=weight_scratch
        + [pltpu.VMEM((rows, hidden_width), bf16), pltpu.SemaphoreType.DMA((2,))],
        name="backward",
    )(where, grad_out, hidden, grad_logit[:, None], router_row, *arrays)
    tail = jnp.concatenate([high, middle, low, jnp.zeros((5, width), bf16)], axis=0)
    tail = jnp.broadcast_to(tail[None], (experts,) + tail.shape)
    back = lax.dynamic_update_slice(back, tail, (0, capacity, 0))
    back = lax.all_to_all(back, GROUP, 0, 0, tiled=True)
    d_tokens = lax.dot_general(
        picks,
        back[:, :capacity].reshape(slot_total, width),
        (((0,), (0,)), ((), ())),
        preferred_element_type=f32,
    ).astype(bf16)
    router_grad = jnp.sum(back[:, capacity : capacity + 3].astype(f32), axis=1).T

    text_pulls = temper * lax.dot_general(
        pulls, units, (((0,), (0,)), ((), ())), precision=highest
    )
    own_pull = lax.dynamic_slice_in_dim(text_pulls, me * images, images)
    old_pull = lax.dynamic_slice_in_dim(text_pulls, pictures + me * images, images)
    own_unit = lax.dynamic_slice_in_dim(text_units, me * images, images)
    own_scale = lax.dynamic_slice_in_dim(text_scales, me * images, images)
    grad_text = own_pull + lax.ppermute(
        old_pull, DP, [((i + 1) % 64, i) for i in range(64)]
    )
    d_texts = (
        grad_text - own_unit * jnp.sum(own_unit * grad_text, axis=1, keepdims=True)
    ) * own_scale
    return d_tokens, d_texts, router_grad


def solution(mesh):
    fine = Mesh(mesh.devices.reshape(2, 2, 8, 2, 4, 2), AXES)
    block = P(AXES, None)
    flat = P(AXES)
    in_specs = (
        block,
        flat,
        flat,
        P(),
        P(("x", "zh"), DP, None),
        P(("x", "zh"), None, DP),
        block,
    )
    out_specs = (block, block, P())
    return jax.shard_map(body, mesh=fine, in_specs=in_specs, out_specs=out_specs, check_vma=False)
```

```python
import functools

import jax
import jax.numpy as jnp
from jax import lax
from jax.experimental import pallas as pl
from jax.experimental.pallas import tpu as pltpu
from jax.sharding import Mesh
from jax.sharding import PartitionSpec as P


highest = lax.Precision.HIGHEST
temper = 10.0
offset = -2.0
loss_scale = 256.0
epsilon = 1e-06

AXES = ("a", "b", "y", "c", "x", "zh")
DP = ("a", "b", "y", "c")
GROUP = ("x", "b")
OWNERS = ("a", "y", "c", "zh")
RING = ("a", "b", "zh")

ANY = pl.BlockSpec(memory_space=pl.ANY)
VMEM = pl.BlockSpec(memory_space=pltpu.VMEM)
SMEM = pl.BlockSpec(memory_space=pltpu.SMEM)


def ring_index(z):
    return (z // 2) % 2 * 4 + z % 2 * 2 + z // 4


def depth_round(k):
    return [
        (ring_index(4 * p + i), ring_index(2 * ((i + k) % 4) + p))
        for p in range(2)
        for i in range(4)
    ]


def ring_step(d):
    return [(i, (i + d) % 8) for i in range(8)]


def swap_cores(block):
    return lax.ppermute(block, "c", [(0, 1), (1, 0)])


def contract_last(left, right):
    return lax.dot_general(
        left, right, (((1,), (1,)), ((), ())), preferred_element_type=jnp.float32
    )


def start_copies(where, parts, refs, w_ref, sem, kind):
    y, j, c = where[0], where[1], where[2]
    for which, lead, k, far, other in parts:
        at_y = lax.rem(y + far, 8)
        at_zl = lax.rem(j - k + 4, 4)
        core = 1 - c if other else c
        row = pl.multiple_of(((at_zl * 8 + at_y) * 2 + core) * 16, 16)
        src = refs[which].at[lead, pl.ds(kind * 16, 16), :]
        pltpu.make_async_copy(src, w_ref.at[pl.ds(row, 16), :], sem).start()


def wait_all(w_ref, sem):
    pltpu.make_async_copy(w_ref, w_ref, sem).wait()


def forward_kernel(parts, count, where, x_ref, mix_ref, *rest):
    refs, (hid_ref, out_ref, part_ref, win, wout, act, sems) = rest[:count], rest[count:]
    start_copies(where, parts, refs, win, sems.at[0], 0)
    start_copies(where, parts, refs, wout, sems.at[1], 1)
    wait_all(win, sems.at[0])
    for n in range(4):
        at = slice(n * 512, n * 512 + 512)
        hidden = jnp.dot(x_ref[...], win[:, at], preferred_element_type=jnp.float32)
        hid_ref[:, at] = hidden
        act[:, at] = jax.nn.gelu(hidden, approximate=True).astype(jnp.bfloat16)
    wait_all(wout, sems.at[1])
    for n in range(4):
        at = slice(n * 256, n * 256 + 256)
        out = contract_last(act[...], wout[at, :]).astype(jnp.bfloat16)
        out_ref[:, at] = out
        part = jnp.dot(
            mix_ref[...],
            out.astype(jnp.float32),
            precision=highest,
            preferred_element_type=jnp.float32,
        ).astype(jnp.bfloat16)
        for member in range(part_ref.shape[0]):
            part_ref[member, :, at] = part


def gelu_slope(hidden):
    scale = 0.7978845608028654
    square = hidden * hidden
    bent = jnp.tanh(scale * (hidden + 0.044715 * (square * hidden)))
    inner = scale * (1.0 + 3.0 * 0.044715 * square)
    return 0.5 * (1.0 + bent) + 0.5 * hidden * (1.0 - bent * bent) * inner


def backward_kernel(parts, count, where, dy_ref, hid_ref, grad_logit, router_row, *rest):
    refs, (back_ref, win, wout, dhid, sems) = rest[:count], rest[count:]
    start_copies(where, parts, refs, wout, sems.at[1], 1)
    start_copies(where, parts, refs, win, sems.at[0], 0)
    wait_all(wout, sems.at[1])
    for n in range(4):
        at = slice(n * 512, n * 512 + 512)
        grad = jnp.dot(dy_ref[...], wout[:, at], preferred_element_type=jnp.float32)
        dhid[:, at] = (grad * gelu_slope(hid_ref[:, at])).astype(jnp.bfloat16)
    wait_all(win, sems.at[0])
    members, _, width = back_ref.shape
    capacity = dhid.shape[0] // members
    back_ref[:, capacity:, :] = jnp.zeros((members, 8, width), jnp.bfloat16)
    for n in range(4):
        at = slice(n * 256, n * 256 + 256)
        moved = contract_last(dhid[...], win[at, :]).astype(jnp.bfloat16)
        rows = moved.astype(jnp.float32) + grad_logit[...] * router_row[:, at]
        for member in range(members):
            block = rows[member * capacity : (member + 1) * capacity]
            back_ref[member, :capacity, at] = block.astype(jnp.bfloat16)


def gathered_weights(w_in, w_out, settle):
    own = jnp.concatenate([w_in[0], w_out[0].T], axis=0)
    rounds = [lax.ppermute(own, RING, depth_round(k)) for k in range(4)]
    mine = jnp.stack(rounds)
    arrays, parts = [], []

    def add(array, entries, other):
        parts.extend((len(arrays), i, k, far % 8, other) for i, (k, far) in enumerate(entries))
        arrays.append(array)

    def keep(pool):
        table = []
        for block, ks, far in pool:
            entries = [(k, far) for k in ks]
            add(block, entries, False)
            table.extend(entries)
        blocks = [block for block, _, _ in pool]
        joined = blocks[0] if len(blocks) == 1 else jnp.concatenate(blocks)
        add(swap_cores(joined), table, True)

    every = range(4)
    fresh, up, down = [(mine, every, 0)], mine, mine
    for step in range(1, 5):
        if step == 4:
            up, down, settled = lax.optimization_barrier((up, down, settle()))
            up, down = up[:2], down[2:]
        up = lax.ppermute(up, "y", ring_step(1))
        down = lax.ppermute(down, "y", ring_step(-1))
        keep(fresh)
        fresh = [(up, every, -step), (down, every, step)]
    keep([(up, (0, 1), 4), (down, (2, 3), 4)])
    return arrays, parts, settled


def share(block, axes, count):
    return lax.all_to_all(
        jnp.broadcast_to(block[None], (count,) + block.shape), axes, 0, 0, tiled=True
    )


def unit_rows(matrix):
    scales = lax.rsqrt(jnp.sum(matrix * matrix, axis=1, keepdims=True) + epsilon)
    return matrix * scales, scales


def layer(tokens, expert_ids, slots, router, w_in, w_out, texts):
    tok_count, width = tokens.shape
    experts = router.shape[1]
    capacity = 5 * tok_count // (4 * experts)
    images = texts.shape[0]
    patch = tok_count // images
    slot_total = experts * capacity
    rows = slot_total
    hidden_width = w_in.shape[2]
    f32, bf16 = jnp.float32, jnp.bfloat16
    me = lax.axis_index(GROUP)
    pictures = experts * images

    before = lax.ppermute(texts, DP, [(i, (i + 1) % 64) for i in range(64)])
    places = jnp.where(slots >= 0, expert_ids * capacity + slots, slot_total)
    picks = (jnp.arange(slot_total, dtype=jnp.int32)[:, None] == places[None, :]).astype(bf16)
    image_of = me * images + jnp.arange(tok_count, dtype=jnp.int32) // patch
    marks = (image_of[:, None] == jnp.arange(128, dtype=jnp.int32)[None, :]).astype(bf16)
    wide = jnp.concatenate([tokens, marks], axis=1)
    send = jnp.dot(picks, wide, preferred_element_type=f32).astype(bf16)
    pair = jnp.pad(jnp.concatenate([texts, before], axis=0), ((0, 0), (0, 128)))
    send = jnp.concatenate(
        [
            send.reshape(experts, capacity, width + 128),
            jnp.broadcast_to(pair[None], (experts,) + pair.shape),
        ],
        axis=1,
    )
    mine = (jnp.arange(experts, dtype=jnp.int32) == me).astype(f32)
    y_at, c_at = lax.axis_index("y"), lax.axis_index("c")
    j_at = 2 * lax.axis_index("zh") + lax.axis_index("a")
    place = jnp.arange(3, dtype=jnp.int32)
    where = jnp.where(place == 0, y_at, jnp.where(place == 1, j_at, c_at)).astype(jnp.int32)

    def settle():
        arrived = lax.all_to_all(send, GROUP, 0, 0, tiled=True)
        routed = arrived[:, :capacity, :width].reshape(rows, width)
        marked = arrived[:, :capacity, width : width + pictures].reshape(rows, pictures)
        marked = marked.astype(f32)
        own_text = arrived[:, capacity : capacity + images, :width].reshape(pictures, width)
        old_text = arrived[:, capacity + images :, :width].reshape(pictures, width)
        logits = jnp.dot(routed, router, preferred_element_type=f32)
        gates = jax.nn.sigmoid(jnp.sum(logits * mine[None, :], axis=1))
        router_row = jnp.sum(router.astype(f32) * mine[None, :], axis=1)[None, :]
        mix = (marked * gates[:, None]).T
        text_units, text_scales = unit_rows(
            jnp.concatenate([own_text, old_text], axis=0).astype(f32)
        )
        at_row = jnp.arange(pictures, dtype=jnp.int32)[:, None]
        at_col = jnp.arange(2 * pictures, dtype=jnp.int32)[None, :]
        paired = (at_row // images == (at_col % pictures) // images).astype(f32)
        label = (at_row == at_col).astype(f32)
        return routed, marked, gates, router_row, mix, text_units, text_scales, where, paired, label

    arrays, parts, settled = gathered_weights(w_in, w_out, settle)
    routed, marked, gates, router_row, mix, text_units, text_scales, where, paired, label = settled

    weight_scratch = [pltpu.VMEM((width, hidden_width), bf16)] * 2
    hidden, out, part = pl.pallas_call(
        functools.partial(forward_kernel, parts, len(arrays)),
        out_shape=(
            jax.ShapeDtypeStruct((rows, hidden_width), f32),
            jax.ShapeDtypeStruct((rows, width), bf16),
            jax.ShapeDtypeStruct((experts, pictures, width), bf16),
        ),
        in_specs=[SMEM, VMEM, VMEM] + [ANY] * len(arrays),
        out_specs=(VMEM, VMEM, VMEM),
        scratch_shapes=weight_scratch
        + [pltpu.VMEM((rows, hidden_width), bf16), pltpu.SemaphoreType.DMA((2,))],
        name="forward",
    )(where, routed, mix, *arrays)

    shared = lax.all_to_all(part, GROUP, 0, 0, tiled=True)
    out_float = out.astype(f32)
    pooled = jnp.sum(shared.astype(f32), axis=0) / patch

    units, pooled_scale = unit_rows(pooled)
    scores = temper * lax.dot_general(
        units, text_units, (((1,), (1,)), ((), ())), precision=highest
    ) + offset
    pulls = paired * (loss_scale * (jax.nn.sigmoid(scores) - label))
    grad_image = temper * jnp.dot(pulls, text_units, precision=highest)
    grad_pooled = (
        grad_image - units * jnp.sum(units * grad_image, axis=1, keepdims=True)
    ) * pooled_scale
    grad_branch = grad_pooled / patch

    spread = jnp.dot(marked, grad_branch, precision=highest)
    grad_out = (gates[:, None] * spread).astype(bf16)
    grad_gate = jnp.sum(spread * out_float, axis=1)
    grad_logit = grad_gate * gates * (1.0 - gates)
    column = jnp.dot(grad_logit[None, :], routed.astype(f32), precision=highest)
    columns = share(column.reshape(8, width // 8), OWNERS, 64)
    column = jnp.sum(columns, axis=0).reshape(1, width)
    high = column.astype(bf16)
    rest = column - high.astype(f32)
    middle = rest.astype(bf16)
    low = (rest - middle.astype(f32)).astype(bf16)

    back = pl.pallas_call(
        functools.partial(backward_kernel, parts, len(arrays)),
        out_shape=jax.ShapeDtypeStruct((experts, capacity + 8, width), bf16),
        in_specs=[SMEM, VMEM, VMEM, VMEM, VMEM] + [ANY] * len(arrays),
        out_specs=VMEM,
        scratch_shapes=weight_scratch
        + [pltpu.VMEM((rows, hidden_width), bf16), pltpu.SemaphoreType.DMA((2,))],
        name="backward",
    )(where, grad_out, hidden, grad_logit[:, None], router_row, *arrays)
    tail = jnp.concatenate([high, middle, low, jnp.zeros((5, width), bf16)], axis=0)
    tail = jnp.broadcast_to(tail[None], (experts,) + tail.shape)
    back = lax.dynamic_update_slice(back, tail, (0, capacity, 0))
    back = lax.all_to_all(back, GROUP, 0, 0, tiled=True)
    d_tokens = lax.dot_general(
        picks,
        back[:, :capacity].reshape(slot_total, width),
        (((0,), (0,)), ((), ())),
        preferred_element_type=f32,
    ).astype(bf16)
    router_grad = jnp.sum(back[:, capacity : capacity + 3].astype(f32), axis=1).T

    text_pulls = temper * lax.dot_general(
        pulls, units, (((0,), (0,)), ((), ())), precision=highest
    )
    own_pull = lax.dynamic_slice_in_dim(text_pulls, me * images, images)
    old_pull = lax.dynamic_slice_in_dim(text_pulls, pictures + me * images, images)
    own_unit = lax.dynamic_slice_in_dim(text_units, me * images, images)
    own_scale = lax.dynamic_slice_in_dim(text_scales, me * images, images)
    grad_text = own_pull + lax.ppermute(
        old_pull, DP, [((i + 1) % 64, i) for i in range(64)]
    )
    d_texts = (
        grad_text - own_unit * jnp.sum(own_unit * grad_text, axis=1, keepdims=True)
    ) * own_scale
    return d_tokens, d_texts, router_grad


def solution(mesh):
    fine = Mesh(mesh.devices.reshape(2, 2, 8, 2, 4, 2), AXES)
    block = P(AXES, None)
    flat = P(AXES)
    in_specs = (
        block,
        flat,
        flat,
        P(),
        P(("x", "zh"), DP, None),
        P(("x", "zh"), None, DP),
        block,
    )
    out_specs = (block, block, P())
    return jax.shard_map(layer, mesh=fine, in_specs=in_specs, out_specs=out_specs, check_vma=False)
```

```python
import functools

import jax
import jax.numpy as jnp
from jax import lax
from jax.experimental import pallas as pl
from jax.experimental.pallas import tpu as pltpu
from jax.sharding import Mesh
from jax.sharding import PartitionSpec as P


highest = lax.Precision.HIGHEST
temper = 10.0
offset = -2.0
loss_scale = 256.0
epsilon = 1e-06

AXES = ("a", "b", "y", "c", "x", "zh")
DP = ("a", "b", "y", "c")
GROUP = ("x", "b")
OWNERS = ("a", "y", "c", "zh")
DEEP = ("a", "b", "c", "zh")

ANY = pl.BlockSpec(memory_space=pl.ANY)
VMEM = pl.BlockSpec(memory_space=pltpu.VMEM)
SMEM = pl.BlockSpec(memory_space=pltpu.SMEM)


def deep_index(z, core):
    return ((z // 2) % 2 * 2 + z % 2) * 4 + core * 2 + z // 4


def depth_round(n):
    route = []
    for core in range(2):
        for p in range(2):
            for i in range(4):
                start, end = 4 * p + i, 2 * ((i + 2 * core + n) % 4) + p
                route.append((deep_index(start, core), deep_index(end, core)))
    return route


def ring_route():
    up = [(2 * y, 2 * ((y + 1) % 8)) for y in range(8)]
    down = [(2 * y + 1, 2 * ((y - 1) % 8) + 1) for y in range(8)]
    return up + down


def swap_cores(block):
    return lax.ppermute(block, "c", [(0, 1), (1, 0)])


def contract_last(left, right):
    return lax.dot_general(
        left, right, (((1,), (1,)), ((), ())), preferred_element_type=jnp.float32
    )


def start_copies(where, parts, refs, w_ref, sem, kind):
    y, j, c = where[0], where[1], where[2]
    for ref, (step, swapped, flip) in zip(refs, parts):
        ahead = 2 * c - 1 if not swapped else 1 - 2 * c
        at_y = lax.rem(y + 8 + ahead * step, 8)
        holder = 1 - c if flip else c
        for lead in range(4):
            core = holder if lead % 2 == 0 else 1 - holder
            at_zl = lax.rem(j + 4 - (2 * holder + lead // 2), 4)
            row = pl.multiple_of(((at_zl * 8 + at_y) * 2 + core) * 16, 16)
            src = ref.at[lead, pl.ds(kind * 16, 16), :]
            pltpu.make_async_copy(src, w_ref.at[pl.ds(row, 16), :], sem).start()


def wait_all(w_ref, sem):
    pltpu.make_async_copy(w_ref, w_ref, sem).wait()


def forward_kernel(parts, count, where, x_ref, mix_ref, *rest):
    refs, (hid_ref, out_ref, part_ref, win, wout, act, sems) = rest[:count], rest[count:]
    start_copies(where, parts, refs, win, sems.at[0], 0)
    start_copies(where, parts, refs, wout, sems.at[1], 1)
    wait_all(win, sems.at[0])
    for n in range(4):
        at = slice(n * 512, n * 512 + 512)
        hidden = jnp.dot(x_ref[...], win[:, at], preferred_element_type=jnp.float32)
        hid_ref[:, at] = hidden
        act[:, at] = jax.nn.gelu(hidden, approximate=True).astype(jnp.bfloat16)
    wait_all(wout, sems.at[1])
    for n in range(4):
        at = slice(n * 256, n * 256 + 256)
        out = contract_last(act[...], wout[at, :]).astype(jnp.bfloat16)
        out_ref[:, at] = out
        part = jnp.dot(
            mix_ref[...],
            out.astype(jnp.float32),
            precision=highest,
            preferred_element_type=jnp.float32,
        ).astype(jnp.bfloat16)
        for member in range(part_ref.shape[0]):
            part_ref[member, :, at] = part


def gelu_slope(hidden):
    scale = 0.7978845608028654
    square = hidden * hidden
    bent = jnp.tanh(scale * (hidden + 0.044715 * (square * hidden)))
    inner = scale * (1.0 + 3.0 * 0.044715 * square)
    return 0.5 * (1.0 + bent) + 0.5 * hidden * (1.0 - bent * bent) * inner


def backward_kernel(parts, count, where, dy_ref, hid_ref, grad_logit, router_row, *rest):
    refs, (back_ref, win, wout, dhid, sems) = rest[:count], rest[count:]
    start_copies(where, parts, refs, wout, sems.at[1], 1)
    start_copies(where, parts, refs, win, sems.at[0], 0)
    wait_all(wout, sems.at[1])
    for n in range(4):
        at = slice(n * 512, n * 512 + 512)
        grad = jnp.dot(dy_ref[...], wout[:, at], preferred_element_type=jnp.float32)
        dhid[:, at] = (grad * gelu_slope(hid_ref[:, at])).astype(jnp.bfloat16)
    wait_all(win, sems.at[0])
    members, _, width = back_ref.shape
    capacity = dhid.shape[0] // members
    back_ref[:, capacity:, :] = jnp.zeros((members, 8, width), jnp.bfloat16)
    for n in range(4):
        at = slice(n * 256, n * 256 + 256)
        moved = contract_last(dhid[...], win[at, :]).astype(jnp.bfloat16)
        rows = moved.astype(jnp.float32) + grad_logit[...] * router_row[:, at]
        for member in range(members):
            block = rows[member * capacity : (member + 1) * capacity]
            back_ref[member, :capacity, at] = block.astype(jnp.bfloat16)


def gathered_weights(w_in, w_out, settle):
    own = jnp.concatenate([w_in[0], w_out[0].T], axis=0)
    pair = jnp.stack([own, swap_cores(own)])
    mine = jnp.concatenate([lax.ppermute(pair, DEEP, depth_round(n)) for n in range(2)])
    theirs = swap_cores(mine)
    arrays, parts = [mine, theirs], [(0, False, False), (0, False, True)]
    chunks = [mine, theirs]
    for step in range(1, 5):
        for n in range(2 if step < 4 else 1):
            moved = lax.ppermute(chunks[n], ("y", "c"), ring_route())
            chunks[n] = moved
            arrays.append(moved)
            parts.append((step, False, n == 1))
            if step == 4:
                moved, settled = lax.optimization_barrier((moved, settle()))
            arrays.append(swap_cores(moved))
            parts.append((step, True, n == 0))
    return arrays, parts, settled


def share(block, axes, count):
    return lax.all_to_all(
        jnp.broadcast_to(block[None], (count,) + block.shape), axes, 0, 0, tiled=True
    )


def unit_rows(matrix):
    scales = lax.rsqrt(jnp.sum(matrix * matrix, axis=1, keepdims=True) + epsilon)
    return matrix * scales, scales


def layer(tokens, expert_ids, slots, router, w_in, w_out, texts):
    tok_count, width = tokens.shape
    experts = router.shape[1]
    capacity = 5 * tok_count // (4 * experts)
    images = texts.shape[0]
    patch = tok_count // images
    slot_total = experts * capacity
    rows = slot_total
    hidden_width = w_in.shape[2]
    f32, bf16 = jnp.float32, jnp.bfloat16
    me = lax.axis_index(GROUP)
    pictures = experts * images

    before = lax.ppermute(texts, DP, [(i, (i + 1) % 64) for i in range(64)])
    places = jnp.where(slots >= 0, expert_ids * capacity + slots, slot_total)
    picks = (jnp.arange(slot_total, dtype=jnp.int32)[:, None] == places[None, :]).astype(bf16)
    image_of = me * images + jnp.arange(tok_count, dtype=jnp.int32) // patch
    marks = (image_of[:, None] == jnp.arange(128, dtype=jnp.int32)[None, :]).astype(bf16)
    wide = jnp.concatenate([tokens, marks], axis=1)
    send = jnp.dot(picks, wide, preferred_element_type=f32).astype(bf16)
    pair = jnp.pad(jnp.concatenate([texts, before], axis=0), ((0, 0), (0, 128)))
    send = jnp.concatenate(
        [
            send.reshape(experts, capacity, width + 128),
            jnp.broadcast_to(pair[None], (experts,) + pair.shape),
        ],
        axis=1,
    )
    mine = (jnp.arange(experts, dtype=jnp.int32) == me).astype(f32)
    y_at, c_at = lax.axis_index("y"), lax.axis_index("c")
    j_at = 2 * lax.axis_index("zh") + lax.axis_index("a")
    place = jnp.arange(3, dtype=jnp.int32)
    where = jnp.where(place == 0, y_at, jnp.where(place == 1, j_at, c_at)).astype(jnp.int32)

    def settle():
        arrived = lax.all_to_all(send, GROUP, 0, 0, tiled=True)
        routed = arrived[:, :capacity, :width].reshape(rows, width)
        marked = arrived[:, :capacity, width : width + pictures].reshape(rows, pictures)
        marked = marked.astype(f32)
        own_text = arrived[:, capacity : capacity + images, :width].reshape(pictures, width)
        old_text = arrived[:, capacity + images :, :width].reshape(pictures, width)
        logits = jnp.dot(routed, router, preferred_element_type=f32)
        gates = jax.nn.sigmoid(jnp.sum(logits * mine[None, :], axis=1))
        router_row = jnp.sum(router.astype(f32) * mine[None, :], axis=1)[None, :]
        mix = lax.dot_general(
            jnp.eye(pictures, dtype=f32),
            marked * gates[:, None],
            (((1,), (1,)), ((), ())),
            precision=highest,
        )
        text_units, text_scales = unit_rows(
            jnp.concatenate([own_text, old_text], axis=0).astype(f32)
        )
        at_row = jnp.arange(pictures, dtype=jnp.int32)[:, None]
        at_col = jnp.arange(2 * pictures, dtype=jnp.int32)[None, :]
        paired = (at_row // images == (at_col % pictures) // images).astype(f32)
        label = (at_row == at_col).astype(f32)
        return routed, marked, gates, router_row, mix, text_units, text_scales, where, paired, label

    arrays, parts, settled = gathered_weights(w_in, w_out, settle)
    routed, marked, gates, router_row, mix, text_units, text_scales, where, paired, label = settled

    weight_scratch = [pltpu.VMEM((width, hidden_width), bf16)] * 2
    hidden, out, part = pl.pallas_call(
        functools.partial(forward_kernel, parts, len(arrays)),
        out_shape=(
            jax.ShapeDtypeStruct((rows, hidden_width), f32),
            jax.ShapeDtypeStruct((rows, width), bf16),
            jax.ShapeDtypeStruct((experts, pictures, width), bf16),
        ),
        in_specs=[SMEM, VMEM, VMEM] + [ANY] * len(arrays),
        out_specs=(VMEM, VMEM, VMEM),
        scratch_shapes=weight_scratch
        + [pltpu.VMEM((rows, hidden_width), bf16), pltpu.SemaphoreType.DMA((2,))],
        name="forward",
    )(where, routed, mix, *arrays)

    shared = lax.all_to_all(part, GROUP, 0, 0, tiled=True)
    out_float = out.astype(f32)
    pooled = jnp.sum(shared.astype(f32), axis=0) / patch

    units, pooled_scale = unit_rows(pooled)
    scores = temper * lax.dot_general(
        units, text_units, (((1,), (1,)), ((), ())), precision=highest
    ) + offset
    pulls = paired * (loss_scale * (jax.nn.sigmoid(scores) - label))
    grad_image = temper * jnp.dot(pulls, text_units, precision=highest)
    grad_pooled = (
        grad_image - units * jnp.sum(units * grad_image, axis=1, keepdims=True)
    ) * pooled_scale
    grad_branch = grad_pooled / patch

    spread = jnp.dot(marked, grad_branch, precision=highest)
    grad_out = (gates[:, None] * spread).astype(bf16)
    grad_gate = jnp.sum(spread * out_float, axis=1)
    grad_logit = grad_gate * gates * (1.0 - gates)
    column = jnp.dot(grad_logit[None, :], routed.astype(f32), precision=highest)
    columns = share(column.reshape(8, width // 8), OWNERS, 64)
    column = jnp.sum(columns, axis=0).reshape(1, width)
    high = column.astype(bf16)
    rest = column - high.astype(f32)
    middle = rest.astype(bf16)
    low = (rest - middle.astype(f32)).astype(bf16)

    back = pl.pallas_call(
        functools.partial(backward_kernel, parts, len(arrays)),
        out_shape=jax.ShapeDtypeStruct((experts, capacity + 8, width), bf16),
        in_specs=[SMEM, VMEM, VMEM, VMEM, VMEM] + [ANY] * len(arrays),
        out_specs=VMEM,
        scratch_shapes=weight_scratch
        + [pltpu.VMEM((rows, hidden_width), bf16), pltpu.SemaphoreType.DMA((2,))],
        name="backward",
    )(where, grad_out, hidden, grad_logit[:, None], router_row, *arrays)
    tail = jnp.concatenate([high, middle, low, jnp.zeros((5, width), bf16)], axis=0)
    tail = jnp.broadcast_to(tail[None], (experts,) + tail.shape)
    back = lax.dynamic_update_slice(back, tail, (0, capacity, 0))
    back = lax.all_to_all(back, GROUP, 0, 0, tiled=True)
    d_tokens = lax.dot_general(
        picks,
        back[:, :capacity].reshape(slot_total, width),
        (((0,), (0,)), ((), ())),
        preferred_element_type=f32,
    ).astype(bf16)
    router_grad = jnp.sum(back[:, capacity : capacity + 3].astype(f32), axis=1).T

    text_pulls = temper * lax.dot_general(
        pulls, units, (((0,), (0,)), ((), ())), precision=highest
    )
    own_pull = lax.dynamic_slice_in_dim(text_pulls, me * images, images)
    old_pull = lax.dynamic_slice_in_dim(text_pulls, pictures + me * images, images)
    own_unit = lax.dynamic_slice_in_dim(text_units, me * images, images)
    own_scale = lax.dynamic_slice_in_dim(text_scales, me * images, images)
    grad_text = own_pull + lax.ppermute(
        old_pull, DP, [((i + 1) % 64, i) for i in range(64)]
    )
    d_texts = (
        grad_text - own_unit * jnp.sum(own_unit * grad_text, axis=1, keepdims=True)
    ) * own_scale
    return d_tokens, d_texts, router_grad


def solution(mesh):
    fine = Mesh(mesh.devices.reshape(2, 2, 8, 2, 4, 2), AXES)
    block = P(AXES, None)
    flat = P(AXES)
    in_specs = (
        block,
        flat,
        flat,
        P(),
        P(("x", "zh"), DP, None),
        P(("x", "zh"), None, DP),
        block,
    )
    out_specs = (block, block, P())
    return jax.shard_map(layer, mesh=fine, in_specs=in_specs, out_specs=out_specs, check_vma=False)
```

```python
import functools

import jax
import jax.numpy as jnp
from jax import lax
from jax.experimental import pallas as pl
from jax.experimental.pallas import tpu as pltpu
from jax.sharding import Mesh
from jax.sharding import PartitionSpec as P


highest = lax.Precision.HIGHEST
temper = 10.0
offset = -2.0
loss_scale = 256.0
epsilon = 1e-06

AXES = ("a", "b", "y", "c", "x", "zh")
DP = ("a", "b", "y", "c")
GROUP = ("x", "b")
OWNERS = ("a", "y", "c", "zh")
DEEP = ("a", "b", "c", "zh")

ANY = pl.BlockSpec(memory_space=pl.ANY)
VMEM = pl.BlockSpec(memory_space=pltpu.VMEM)
SMEM = pl.BlockSpec(memory_space=pltpu.SMEM)


def deep_index(z, core):
    return ((z // 2) % 2 * 2 + z % 2) * 4 + core * 2 + z // 4


def depth_round(n):
    route = []
    for core in range(2):
        for p in range(2):
            for i in range(4):
                start, end = 4 * p + i, 2 * ((i + 2 * core + n) % 4) + p
                route.append((deep_index(start, core), deep_index(end, core)))
    return route


def ring_route():
    up = [(2 * y, 2 * ((y + 1) % 8)) for y in range(8)]
    down = [(2 * y + 1, 2 * ((y - 1) % 8) + 1) for y in range(8)]
    return up + down


def swap_cores(block):
    return lax.ppermute(block, "c", [(0, 1), (1, 0)])


def contract_last(left, right):
    return lax.dot_general(
        left, right, (((1,), (1,)), ((), ())), preferred_element_type=jnp.float32
    )


def start_copies(where, parts, refs, w_ref, sem, kind):
    y, j, c = where[0], where[1], where[2]
    for ref, (step, swapped, flip) in zip(refs, parts):
        ahead = 2 * c - 1 if not swapped else 1 - 2 * c
        at_y = lax.rem(y + 8 + ahead * step, 8)
        holder = 1 - c if flip else c
        for lead in range(4):
            core = holder if lead % 2 == 0 else 1 - holder
            at_zl = lax.rem(j + 4 - (2 * holder + lead // 2), 4)
            row = pl.multiple_of(((at_zl * 8 + at_y) * 2 + core) * 16, 16)
            src = ref.at[lead, pl.ds(kind * 16, 16), :]
            pltpu.make_async_copy(src, w_ref.at[pl.ds(row, 16), :], sem).start()


def wait_all(w_ref, sem):
    pltpu.make_async_copy(w_ref, w_ref, sem).wait()


def forward_kernel(parts, count, where, x_ref, mix_ref, *rest):
    refs = rest[:count]
    hid_out, out_ref, part_ref, win, wout, act, hid, sems, hid_sems = rest[count:]
    start_copies(where, parts, refs, win, sems.at[0], 0)
    start_copies(where, parts, refs, wout, sems.at[1], 1)
    wait_all(win, sems.at[0])
    leaving = []
    for n in range(4):
        at = slice(n * 512, n * 512 + 512)
        hidden = jnp.dot(x_ref[...], win[:, at], preferred_element_type=jnp.float32)
        hid[:, at] = hidden
        copy = pltpu.make_async_copy(hid.at[:, at], hid_out.at[:, at], hid_sems.at[n])
        copy.start()
        leaving.append(copy)
        act[:, at] = jax.nn.gelu(hidden, approximate=True).astype(jnp.bfloat16)
    wait_all(wout, sems.at[1])
    pictures = part_ref.shape[1]
    for n in range(4):
        at = slice(n * 256, n * 256 + 256)
        out = contract_last(act[...], wout[at, :]).astype(jnp.bfloat16)
        out_ref[:, at] = out
        thirds = jnp.dot(mix_ref[...], out, preferred_element_type=jnp.float32)
        part = thirds[:pictures] + thirds[pictures : 2 * pictures] + thirds[2 * pictures :]
        part = part.astype(jnp.bfloat16)
        for member in range(part_ref.shape[0]):
            part_ref[member, :, at] = part
    for copy in leaving:
        copy.wait()


def gelu_slope(hidden):
    scale = 0.7978845608028654
    square = hidden * hidden
    bent = jnp.tanh(scale * (hidden + 0.044715 * (square * hidden)))
    inner = scale * (1.0 + 3.0 * 0.044715 * square)
    return 0.5 * (1.0 + bent) + 0.5 * hidden * (1.0 - bent * bent) * inner


def backward_kernel(parts, count, where, dy_ref, hid_in, grad_logit, router_row, *rest):
    refs, (back_ref, win, wout, dhid, hid, sems, hid_sem) = rest[:count], rest[count:]
    start_copies(where, parts, refs, wout, sems.at[1], 1)
    entering = pltpu.make_async_copy(hid_in, hid, hid_sem)
    entering.start()
    start_copies(where, parts, refs, win, sems.at[0], 0)
    wait_all(wout, sems.at[1])
    entering.wait()
    for n in range(4):
        at = slice(n * 512, n * 512 + 512)
        grad = jnp.dot(dy_ref[...], wout[:, at], preferred_element_type=jnp.float32)
        dhid[:, at] = (grad * gelu_slope(hid[:, at])).astype(jnp.bfloat16)
    wait_all(win, sems.at[0])
    members, _, width = back_ref.shape
    capacity = dhid.shape[0] // members
    back_ref[:, capacity:, :] = jnp.zeros((members, 8, width), jnp.bfloat16)
    for n in range(4):
        at = slice(n * 256, n * 256 + 256)
        moved = contract_last(dhid[...], win[at, :]).astype(jnp.bfloat16)
        rows = moved.astype(jnp.float32) + grad_logit[...] * router_row[:, at]
        for member in range(members):
            block = rows[member * capacity : (member + 1) * capacity]
            back_ref[member, :capacity, at] = block.astype(jnp.bfloat16)


def gathered_weights(w_in, w_out, settle):
    own = jnp.concatenate([w_in[0], w_out[0].T], axis=0)
    pair = jnp.stack([own, swap_cores(own)])
    mine = jnp.concatenate([lax.ppermute(pair, DEEP, depth_round(n)) for n in range(2)])
    theirs = swap_cores(mine)
    arrays, parts = [mine, theirs], [(0, False, False), (0, False, True)]
    chunks = [mine, theirs]
    for step in range(1, 5):
        for n in range(2 if step < 4 else 1):
            moved = lax.ppermute(chunks[n], ("y", "c"), ring_route())
            chunks[n] = moved
            arrays.append(moved)
            parts.append((step, False, n == 1))
            if step == 4:
                moved, settled = lax.optimization_barrier((moved, settle()))
            arrays.append(swap_cores(moved))
            parts.append((step, True, n == 0))
    return arrays, parts, settled


def share(block, axes, count):
    return lax.all_to_all(
        jnp.broadcast_to(block[None], (count,) + block.shape), axes, 0, 0, tiled=True
    )


def thirds_of(matrix):
    high = lax.reduce_precision(matrix, 8, 7)
    rest = matrix - high
    middle = lax.reduce_precision(rest, 8, 7)
    return tuple(x.astype(jnp.bfloat16) for x in (high, middle, rest - middle))


def unit_rows(matrix):
    scales = lax.rsqrt(jnp.sum(matrix * matrix, axis=1, keepdims=True) + epsilon)
    return matrix * scales, scales


def layer(tokens, expert_ids, slots, router, w_in, w_out, texts):
    tok_count, width = tokens.shape
    experts = router.shape[1]
    capacity = 5 * tok_count // (4 * experts)
    images = texts.shape[0]
    patch = tok_count // images
    slot_total = experts * capacity
    rows = slot_total
    hidden_width = w_in.shape[2]
    f32, bf16 = jnp.float32, jnp.bfloat16
    me = lax.axis_index(GROUP)
    pictures = experts * images

    before = lax.ppermute(texts, DP, [(i, (i + 1) % 64) for i in range(64)])
    places = jnp.where(slots >= 0, expert_ids * capacity + slots, slot_total)
    picks = (jnp.arange(slot_total, dtype=jnp.int32)[:, None] == places[None, :]).astype(bf16)
    image_of = me * images + jnp.arange(tok_count, dtype=jnp.int32) // patch
    marks = (image_of[:, None] == jnp.arange(128, dtype=jnp.int32)[None, :]).astype(bf16)
    wide = jnp.concatenate([tokens, marks], axis=1)
    send = jnp.dot(picks, wide, preferred_element_type=f32).astype(bf16)
    pair = jnp.pad(jnp.concatenate([texts, before], axis=0), ((0, 0), (0, 128)))
    send = jnp.concatenate(
        [
            send.reshape(experts, capacity, width + 128),
            jnp.broadcast_to(pair[None], (experts,) + pair.shape),
        ],
        axis=1,
    )
    mine = (jnp.arange(experts, dtype=jnp.int32) == me).astype(f32)
    y_at, c_at = lax.axis_index("y"), lax.axis_index("c")
    j_at = 2 * lax.axis_index("zh") + lax.axis_index("a")
    place = jnp.arange(3, dtype=jnp.int32)
    where = jnp.where(place == 0, y_at, jnp.where(place == 1, j_at, c_at)).astype(jnp.int32)

    def settle():
        arrived = lax.all_to_all(send, GROUP, 0, 0, tiled=True)
        routed = arrived[:, :capacity, :width].reshape(rows, width)
        marked = arrived[:, :capacity, width : width + pictures].reshape(rows, pictures)
        marked = marked.astype(f32)
        own_text = arrived[:, capacity : capacity + images, :width].reshape(pictures, width)
        old_text = arrived[:, capacity + images :, :width].reshape(pictures, width)
        logits = jnp.dot(routed, router, preferred_element_type=f32)
        gates = jax.nn.sigmoid(jnp.sum(logits * mine[None, :], axis=1))
        router_row = jnp.sum(router.astype(f32) * mine[None, :], axis=1)[None, :]
        mix = lax.dot_general(
            jnp.eye(pictures, dtype=f32),
            marked * gates[:, None],
            (((1,), (1,)), ((), ())),
            precision=highest,
        )
        mix = jnp.concatenate(thirds_of(mix), axis=0)
        text_units, text_scales = unit_rows(
            jnp.concatenate([own_text, old_text], axis=0).astype(f32)
        )
        at_row = jnp.arange(pictures, dtype=jnp.int32)[:, None]
        at_col = jnp.arange(2 * pictures, dtype=jnp.int32)[None, :]
        paired = (at_row // images == (at_col % pictures) // images).astype(f32)
        label = (at_row == at_col).astype(f32)
        return routed, marked, gates, router_row, mix, text_units, text_scales, where, paired, label

    arrays, parts, settled = gathered_weights(w_in, w_out, settle)
    routed, marked, gates, router_row, mix, text_units, text_scales, where, paired, label = settled

    weight_scratch = [pltpu.VMEM((width, hidden_width), bf16)] * 2
    hidden, out, part = pl.pallas_call(
        functools.partial(forward_kernel, parts, len(arrays)),
        out_shape=(
            jax.ShapeDtypeStruct((rows, hidden_width), f32),
            jax.ShapeDtypeStruct((rows, width), bf16),
            jax.ShapeDtypeStruct((experts, pictures, width), bf16),
        ),
        in_specs=[SMEM, VMEM, VMEM] + [ANY] * len(arrays),
        out_specs=(ANY, VMEM, VMEM),
        scratch_shapes=weight_scratch
        + [
            pltpu.VMEM((rows, hidden_width), bf16),
            pltpu.VMEM((rows, hidden_width), f32),
            pltpu.SemaphoreType.DMA((2,)),
            pltpu.SemaphoreType.DMA((4,)),
        ],
        name="forward",
    )(where, routed, mix, *arrays)

    shared = lax.all_to_all(part, GROUP, 0, 0, tiled=True)
    out_float = out.astype(f32)
    pooled = jnp.sum(shared.astype(f32), axis=0) / patch

    units, pooled_scale = unit_rows(pooled)
    scores = temper * lax.dot_general(
        units, text_units, (((1,), (1,)), ((), ())), precision=highest
    ) + offset
    pulls = paired * (loss_scale * (jax.nn.sigmoid(scores) - label))
    grad_image = temper * jnp.dot(pulls, text_units, precision=highest)
    grad_pooled = (
        grad_image - units * jnp.sum(units * grad_image, axis=1, keepdims=True)
    ) * pooled_scale
    grad_branch = grad_pooled / patch

    spread = jnp.dot(marked, grad_branch, precision=highest)
    grad_out = (gates[:, None] * spread).astype(bf16)
    grad_gate = jnp.sum(spread * out_float, axis=1)
    grad_logit = grad_gate * gates * (1.0 - gates)
    column = jnp.dot(grad_logit[None, :], routed.astype(f32), precision=highest)
    columns = share(column.reshape(8, width // 8), OWNERS, 64)
    column = jnp.sum(columns, axis=0).reshape(1, width)
    high, middle, low = thirds_of(column)

    back = pl.pallas_call(
        functools.partial(backward_kernel, parts, len(arrays)),
        out_shape=jax.ShapeDtypeStruct((experts, capacity + 8, width), bf16),
        in_specs=[SMEM, VMEM, ANY, VMEM, VMEM] + [ANY] * len(arrays),
        out_specs=VMEM,
        scratch_shapes=weight_scratch
        + [
            pltpu.VMEM((rows, hidden_width), bf16),
            pltpu.VMEM((rows, hidden_width), f32),
            pltpu.SemaphoreType.DMA((2,)),
            pltpu.SemaphoreType.DMA,
        ],
        name="backward",
    )(where, grad_out, hidden, grad_logit[:, None], router_row, *arrays)
    tail = jnp.concatenate([high, middle, low, jnp.zeros((5, width), bf16)], axis=0)
    tail = jnp.broadcast_to(tail[None], (experts,) + tail.shape)
    back = lax.dynamic_update_slice(back, tail, (0, capacity, 0))
    back = lax.all_to_all(back, GROUP, 0, 0, tiled=True)
    d_tokens = lax.dot_general(
        picks,
        back[:, :capacity].reshape(slot_total, width),
        (((0,), (0,)), ((), ())),
        preferred_element_type=f32,
    ).astype(bf16)
    router_grad = jnp.sum(back[:, capacity : capacity + 3].astype(f32), axis=1).T

    text_pulls = temper * lax.dot_general(
        pulls, units, (((0,), (0,)), ((), ())), precision=highest
    )
    own_pull = lax.dynamic_slice_in_dim(text_pulls, me * images, images)
    old_pull = lax.dynamic_slice_in_dim(text_pulls, pictures + me * images, images)
    own_unit = lax.dynamic_slice_in_dim(text_units, me * images, images)
    own_scale = lax.dynamic_slice_in_dim(text_scales, me * images, images)
    grad_text = own_pull + lax.ppermute(
        old_pull, DP, [((i + 1) % 64, i) for i in range(64)]
    )
    d_texts = (
        grad_text - own_unit * jnp.sum(own_unit * grad_text, axis=1, keepdims=True)
    ) * own_scale
    return d_tokens, d_texts, router_grad


def solution(mesh):
    fine = Mesh(mesh.devices.reshape(2, 2, 8, 2, 4, 2), AXES)
    block = P(AXES, None)
    flat = P(AXES)
    in_specs = (
        block,
        flat,
        flat,
        P(),
        P(("x", "zh"), DP, None),
        P(("x", "zh"), None, DP),
        block,
    )
    out_specs = (block, block, P())
    return jax.shard_map(layer, mesh=fine, in_specs=in_specs, out_specs=out_specs, check_vma=False)
```

```python
import functools

import jax
import jax.numpy as jnp
from jax import lax
from jax.experimental import pallas as pl
from jax.experimental.pallas import tpu as pltpu
from jax.sharding import Mesh
from jax.sharding import PartitionSpec as P


highest = lax.Precision.HIGHEST
temper = 10.0
offset = -2.0
loss_scale = 256.0
epsilon = 1e-06

AXES = ("a", "b", "y", "c", "x", "zh")
DP = ("a", "b", "y", "c")
GROUP = ("x", "b")
OWNERS = ("a", "y", "c", "zh")
DEEP = ("a", "b", "c", "zh")

ANY = pl.BlockSpec(memory_space=pl.ANY)
VMEM = pl.BlockSpec(memory_space=pltpu.VMEM)
SMEM = pl.BlockSpec(memory_space=pltpu.SMEM)


def deep_index(z, core):
    return ((z // 2) % 2 * 2 + z % 2) * 4 + core * 2 + z // 4


def depth_round(n):
    route = []
    for core in range(2):
        for p in range(2):
            for i in range(4):
                start, end = 4 * p + i, 2 * ((i + 2 * core + n) % 4) + p
                route.append((deep_index(start, core), deep_index(end, core)))
    return route


def ring_route():
    up = [(2 * y, 2 * ((y + 1) % 8)) for y in range(8)]
    down = [(2 * y + 1, 2 * ((y - 1) % 8) + 1) for y in range(8)]
    return up + down


def swap_cores(block):
    return lax.ppermute(block, "c", [(0, 1), (1, 0)])


def contract_last(left, right):
    return lax.dot_general(
        left, right, (((1,), (1,)), ((), ())), preferred_element_type=jnp.float32
    )


def start_copies(where, parts, refs, w_ref, sem, kind):
    y, j, c = where[0], where[1], where[2]
    for ref, (step, swapped, flip) in zip(refs, parts):
        ahead = 2 * c - 1 if not swapped else 1 - 2 * c
        at_y = lax.rem(y + 8 + ahead * step, 8)
        holder = 1 - c if flip else c
        for lead in range(4):
            core = holder if lead % 2 == 0 else 1 - holder
            at_zl = lax.rem(j + 4 - (2 * holder + lead // 2), 4)
            row = pl.multiple_of(((at_zl * 8 + at_y) * 2 + core) * 16, 16)
            src = ref.at[lead, pl.ds(kind * 16, 16), :]
            pltpu.make_async_copy(src, w_ref.at[pl.ds(row, 16), :], sem).start()


def wait_all(w_ref, sem):
    pltpu.make_async_copy(w_ref, w_ref, sem).wait()


def forward_kernel(parts, count, where, x_ref, mix_ref, *rest):
    refs = rest[:count]
    hid_out, out_ref, part_ref, win, wout, act, hid, sems, hid_sems = rest[count:]
    start_copies(where, parts, refs, win, sems.at[0], 0)
    wait_all(win, sems.at[0])
    start_copies(where, parts, refs, wout, sems.at[1], 1)
    leaving = []
    for n in range(4):
        at = slice(n * 512, n * 512 + 512)
        hidden = jnp.dot(x_ref[...], win[:, at], preferred_element_type=jnp.float32)
        hid[:, at] = hidden
        copy = pltpu.make_async_copy(hid.at[:, at], hid_out.at[:, at], hid_sems.at[n])
        copy.start()
        leaving.append(copy)
        act[:, at] = jax.nn.gelu(hidden, approximate=True).astype(jnp.bfloat16)
    wait_all(wout, sems.at[1])
    pictures = part_ref.shape[1]
    for n in range(4):
        at = slice(n * 256, n * 256 + 256)
        out = contract_last(act[...], wout[at, :]).astype(jnp.bfloat16)
        out_ref[:, at] = out
        thirds = jnp.dot(mix_ref[...], out, preferred_element_type=jnp.float32)
        part = thirds[:pictures] + thirds[pictures : 2 * pictures] + thirds[2 * pictures :]
        part = part.astype(jnp.bfloat16)
        for member in range(part_ref.shape[0]):
            part_ref[member, :, at] = part
    for copy in leaving:
        copy.wait()


def gelu_slope(hidden):
    scale = 0.7978845608028654
    square = hidden * hidden
    bent = jnp.tanh(scale * (hidden + 0.044715 * (square * hidden)))
    inner = scale * (1.0 + 3.0 * 0.044715 * square)
    return 0.5 * (1.0 + bent) + 0.5 * hidden * (1.0 - bent * bent) * inner


def backward_kernel(parts, count, where, dy_ref, hid_ref, grad_logit, router_row, *rest):
    refs, (back_ref, win, wout, dhid, sems) = rest[:count], rest[count:]
    start_copies(where, parts, refs, wout, sems.at[1], 1)
    wait_all(wout, sems.at[1])
    start_copies(where, parts, refs, win, sems.at[0], 0)
    for n in range(4):
        at = slice(n * 512, n * 512 + 512)
        grad = jnp.dot(dy_ref[...], wout[:, at], preferred_element_type=jnp.float32)
        dhid[:, at] = (grad * gelu_slope(hid_ref[:, at])).astype(jnp.bfloat16)
    wait_all(win, sems.at[0])
    members, _, width = back_ref.shape
    capacity = dhid.shape[0] // members
    back_ref[:, capacity:, :] = jnp.zeros((members, 8, width), jnp.bfloat16)
    for n in range(4):
        at = slice(n * 256, n * 256 + 256)
        moved = contract_last(dhid[...], win[at, :]).astype(jnp.bfloat16)
        rows = moved.astype(jnp.float32) + grad_logit[...] * router_row[:, at]
        for member in range(members):
            block = rows[member * capacity : (member + 1) * capacity]
            back_ref[member, :capacity, at] = block.astype(jnp.bfloat16)


def gathered_weights(w_in, w_out, settle):
    own = jnp.concatenate([w_in[0], w_out[0].T], axis=0)
    pair = jnp.stack([own, swap_cores(own)])
    mine = jnp.concatenate([lax.ppermute(pair, DEEP, depth_round(n)) for n in range(2)])
    theirs = swap_cores(mine)
    arrays, parts = [mine, theirs], [(0, False, False), (0, False, True)]
    chunks = [mine, theirs]
    for step in range(1, 5):
        for n in range(2 if step < 4 else 1):
            moved = lax.ppermute(chunks[n], ("y", "c"), ring_route())
            chunks[n] = moved
            arrays.append(moved)
            parts.append((step, False, n == 1))
            if step == 4:
                moved, settled, arrays[-2] = lax.optimization_barrier(
                    (moved, settle(), arrays[-2])
                )
            arrays.append(swap_cores(moved))
            parts.append((step, True, n == 0))
    return arrays, parts, settled


def share(block, axes, count):
    return lax.all_to_all(
        jnp.broadcast_to(block[None], (count,) + block.shape), axes, 0, 0, tiled=True
    )


def thirds_of(matrix):
    high = lax.reduce_precision(matrix, 8, 7)
    rest = matrix - high
    middle = lax.reduce_precision(rest, 8, 7)
    return tuple(x.astype(jnp.bfloat16) for x in (high, middle, rest - middle))


def unit_rows(matrix):
    scales = lax.rsqrt(jnp.sum(matrix * matrix, axis=1, keepdims=True) + epsilon)
    return matrix * scales, scales


def layer(tokens, expert_ids, slots, router, w_in, w_out, texts):
    tok_count, width = tokens.shape
    experts = router.shape[1]
    capacity = 5 * tok_count // (4 * experts)
    images = texts.shape[0]
    patch = tok_count // images
    slot_total = experts * capacity
    rows = slot_total
    hidden_width = w_in.shape[2]
    f32, bf16 = jnp.float32, jnp.bfloat16
    me = lax.axis_index(GROUP)
    pictures = experts * images

    before = lax.ppermute(texts, DP, [(i, (i + 1) % 64) for i in range(64)])
    places = jnp.where(slots >= 0, expert_ids * capacity + slots, slot_total)
    picks = (jnp.arange(slot_total, dtype=jnp.int32)[:, None] == places[None, :]).astype(bf16)
    image_of = me * images + jnp.arange(tok_count, dtype=jnp.int32) // patch
    marks = (image_of[:, None] == jnp.arange(128, dtype=jnp.int32)[None, :]).astype(bf16)
    wide = jnp.concatenate([tokens, marks], axis=1)
    send = jnp.dot(picks, wide, preferred_element_type=f32).astype(bf16)
    pair = jnp.pad(jnp.concatenate([texts, before], axis=0), ((0, 0), (0, 128)))
    send = jnp.concatenate(
        [
            send.reshape(experts, capacity, width + 128),
            jnp.broadcast_to(pair[None], (experts,) + pair.shape),
        ],
        axis=1,
    )
    mine = (jnp.arange(experts, dtype=jnp.int32) == me).astype(f32)
    y_at, c_at = lax.axis_index("y"), lax.axis_index("c")
    j_at = 2 * lax.axis_index("zh") + lax.axis_index("a")
    place = jnp.arange(3, dtype=jnp.int32)
    where = jnp.where(place == 0, y_at, jnp.where(place == 1, j_at, c_at)).astype(jnp.int32)

    def settle():
        arrived = lax.all_to_all(send, GROUP, 0, 0, tiled=True)
        routed = arrived[:, :capacity, :width].reshape(rows, width)
        marked = arrived[:, :capacity, width : width + pictures].reshape(rows, pictures)
        marked = marked.astype(f32)
        own_text = arrived[:, capacity : capacity + images, :width].reshape(pictures, width)
        old_text = arrived[:, capacity + images :, :width].reshape(pictures, width)
        logits = jnp.dot(routed, router, preferred_element_type=f32)
        gates = jax.nn.sigmoid(jnp.sum(logits * mine[None, :], axis=1))
        router_row = jnp.sum(router.astype(f32) * mine[None, :], axis=1)[None, :]
        mix = lax.dot_general(
            jnp.eye(pictures, dtype=f32),
            marked * gates[:, None],
            (((1,), (1,)), ((), ())),
            precision=highest,
        )
        mix = jnp.concatenate(thirds_of(mix), axis=0)
        text_units, text_scales = unit_rows(
            jnp.concatenate([own_text, old_text], axis=0).astype(f32)
        )
        at_row = jnp.arange(pictures, dtype=jnp.int32)[:, None]
        at_col = jnp.arange(2 * pictures, dtype=jnp.int32)[None, :]
        paired = (at_row // images == (at_col % pictures) // images).astype(f32)
        label = (at_row == at_col).astype(f32)
        return routed, marked, gates, router_row, mix, text_units, text_scales, where, paired, label

    arrays, parts, settled = gathered_weights(w_in, w_out, settle)
    routed, marked, gates, router_row, mix, text_units, text_scales, where, paired, label = settled

    weight_scratch = [pltpu.VMEM((width, hidden_width), bf16)] * 2
    hidden, out, part = pl.pallas_call(
        functools.partial(forward_kernel, parts, len(arrays)),
        out_shape=(
            jax.ShapeDtypeStruct((rows, hidden_width), f32),
            jax.ShapeDtypeStruct((rows, width), bf16),
            jax.ShapeDtypeStruct((experts, pictures, width), bf16),
        ),
        in_specs=[SMEM, VMEM, VMEM] + [ANY] * len(arrays),
        out_specs=(ANY, VMEM, VMEM),
        scratch_shapes=weight_scratch
        + [
            pltpu.VMEM((rows, hidden_width), bf16),
            pltpu.VMEM((rows, hidden_width), f32),
            pltpu.SemaphoreType.DMA((2,)),
            pltpu.SemaphoreType.DMA((4,)),
        ],
        name="forward",
    )(where, routed, mix, *arrays)

    shared = lax.all_to_all(part, GROUP, 0, 0, tiled=True)
    out_float = out.astype(f32)
    pooled = jnp.sum(shared.astype(f32), axis=0) / patch

    units, pooled_scale = unit_rows(pooled)
    scores = temper * lax.dot_general(
        units, text_units, (((1,), (1,)), ((), ())), precision=highest
    ) + offset
    pulls = paired * (loss_scale * (jax.nn.sigmoid(scores) - label))
    grad_image = temper * jnp.dot(pulls, text_units, precision=highest)
    grad_pooled = (
        grad_image - units * jnp.sum(units * grad_image, axis=1, keepdims=True)
    ) * pooled_scale
    grad_branch = grad_pooled / patch

    spread = jnp.dot(marked, grad_branch, precision=highest)
    grad_out = (gates[:, None] * spread).astype(bf16)
    grad_gate = jnp.sum(spread * out_float, axis=1)
    grad_logit = grad_gate * gates * (1.0 - gates)
    column = jnp.dot(grad_logit[None, :], routed.astype(f32), precision=highest)
    columns = share(column.reshape(8, width // 8), OWNERS, 64)
    column = jnp.sum(columns, axis=0).reshape(1, width)
    high, middle, low = thirds_of(column)

    back = pl.pallas_call(
        functools.partial(backward_kernel, parts, len(arrays)),
        out_shape=jax.ShapeDtypeStruct((experts, capacity + 8, width), bf16),
        in_specs=[SMEM, VMEM, VMEM, VMEM, VMEM] + [ANY] * len(arrays),
        out_specs=VMEM,
        scratch_shapes=weight_scratch
        + [pltpu.VMEM((rows, hidden_width), bf16), pltpu.SemaphoreType.DMA((2,))],
        name="backward",
    )(where, grad_out, hidden, grad_logit[:, None], router_row, *arrays)
    tail = jnp.concatenate([high, middle, low, jnp.zeros((5, width), bf16)], axis=0)
    tail = jnp.broadcast_to(tail[None], (experts,) + tail.shape)
    back = lax.dynamic_update_slice(back, tail, (0, capacity, 0))
    back = lax.all_to_all(back, GROUP, 0, 0, tiled=True)
    d_tokens = lax.dot_general(
        picks,
        back[:, :capacity].reshape(slot_total, width),
        (((0,), (0,)), ((), ())),
        preferred_element_type=f32,
    ).astype(bf16)
    router_grad = jnp.sum(back[:, capacity : capacity + 3].astype(f32), axis=1).T

    text_pulls = temper * lax.dot_general(
        pulls, units, (((0,), (0,)), ((), ())), precision=highest
    )
    own_pull = lax.dynamic_slice_in_dim(text_pulls, me * images, images)
    old_pull = lax.dynamic_slice_in_dim(text_pulls, pictures + me * images, images)
    own_unit = lax.dynamic_slice_in_dim(text_units, me * images, images)
    own_scale = lax.dynamic_slice_in_dim(text_scales, me * images, images)
    grad_text = own_pull + lax.ppermute(
        old_pull, DP, [((i + 1) % 64, i) for i in range(64)]
    )
    d_texts = (
        grad_text - own_unit * jnp.sum(own_unit * grad_text, axis=1, keepdims=True)
    ) * own_scale
    return d_tokens, d_texts, router_grad


def solution(mesh):
    fine = Mesh(mesh.devices.reshape(2, 2, 8, 2, 4, 2), AXES)
    block = P(AXES, None)
    flat = P(AXES)
    in_specs = (
        block,
        flat,
        flat,
        P(),
        P(("x", "zh"), DP, None),
        P(("x", "zh"), None, DP),
        block,
    )
    out_specs = (block, block, P())
    return jax.shard_map(layer, mesh=fine, in_specs=in_specs, out_specs=out_specs, check_vma=False)
```
